32 devices in a mesh: row: 1, voc: 32 (over z, y, x, core).
Axes of the slice: x: 2, y: 2, z: 4, core: 2. Of those that a mesh axis runs over, the one named last changes fastest.
Arguments:
- hidden_states: bfloat16 [256, 4096], P('row'), may hold values from -72 to 72
- student_head: bfloat16 [4096, 65536], P('row', 'voc'), may hold values from -2 to 2
- teacher_probs: bfloat16 [256, 81920], P('row', 'voc'), may hold values from 9.9658966e-05 to 1
- block_map: int32 [512, 2], replicated, may hold values from 0 to 639, as said below
- context: int32 [4], P('row'), may hold values from 0 to 3
- map_gates: float32 [4, 512, 2], P(None, 'voc'), may hold values from 0.2 to 5
- map_tiles: bfloat16 [512, 2, 128, 128], P('voc'), may hold values from 0.0009994507 to 1
Outputs:
- grad_logits: bfloat16 [256, 65536], P('row', 'voc')
- head_grad: bfloat16 [4096, 65536], P('row', 'voc')
- kl_loss: float32 [], replicated
The draws below stay inside these ranges and needn't reach their ends.
Inputs may be any that keep to these rules, and one draw needn't show every extreme that they name: `block_map`: in each aligned block of 16 student blocks, at most 2 of the 32 listed ids lie in any one aligned range of 20 teacher blocks, and exactly 2 in one such range.
All inputs are finite; a program needn't handle non-finite values.
Results may differ from the reference program's by a relative error of at most 0.013.
Values may be sent and summed in bfloat16 or wider, within the bound.
A program may use at most 128 MiB of HBM per device.

```python
import math
import jax
import jax.numpy as jnp
from jax import lax

D = 4096
VS = 65536
VT = 81920
BLK = 128
K = 2
NCTX = 4
WIN = 64
TOK_DEV = 256
TOKENS = 256
NBS = 512
NBT = 640
BS_DEV = 16
BT_DEV = 20
NWIN = 4
N_ROW = 1


def draw_hidden_states(key, part):
    values = jax.random.truncated_normal(key, -6.0, 6.0, (TOKENS, D), jnp.float32)
    token_index = jnp.arange(TOKENS, dtype=jnp.int32)
    aligned = token_index % 16 == 5
    level = token_index // 16 % 3
    strength = jnp.where(level == 0, 13.0, jnp.where(level == 1, 20.0, 30.0)).astype(jnp.float32)
    lead = jnp.arange(D, dtype=jnp.int32) < min(8, D)
    chosen = aligned[:, None] & lead[None, :]
    values = jnp.where(chosen, strength[:, None] * jnp.ones((1, D), jnp.float32), values)
    return values.astype(jnp.bfloat16)


def draw_student_head(key, part):
    noise = jax.random.truncated_normal(key, -6.0, 6.0, (D, VS), jnp.float32) * D ** (-0.5)
    lead = (jnp.arange(D, dtype=jnp.int32) < min(8, D))[:, None]
    values = jnp.where(lead, 1.0 + 0.1 * noise, noise)
    return values.astype(jnp.bfloat16)


def draw_block_map(key, part):
    shard_count = NBS // BS_DEV
    entries = BS_DEV * K
    base_count = entries // shard_count
    rank_counts = jnp.full((shard_count,), base_count, jnp.int32)
    rank_counts = rank_counts.at[0].add(1).at[1].add(-1)

    def one_shard(shard):
        shard_key = jax.random.fold_in(key, shard)
        first_key, second_key, third_key = jax.random.split(shard_key, 3)
        source_order = jax.random.permutation(first_key, shard_count)
        source_rank = jnp.repeat(jnp.arange(shard_count, dtype=jnp.int32), rank_counts, total_repeat_length=entries)
        sources = jax.random.permutation(second_key, source_order[source_rank])
        within = jax.random.randint(third_key, (entries,), 0, BT_DEV)
        return (sources * BT_DEV + within).reshape(BS_DEV, K)
    result = jax.vmap(one_shard)(jnp.arange(shard_count, dtype=jnp.int32))
    return result.reshape(NBS, K).astype(jnp.int32)


def plant(values, own_key, low, largest):
    longest = values.shape.index(max(values.shape))
    spots = []
    for shift in (0, 1):
        where = [jax.random.randint(jax.random.fold_in(own_key, axis), (), 0, length) for axis, length in enumerate(values.shape)]
        where[longest] = (where[longest] + shift) % values.shape[longest]
        spots.append(tuple(where))
    return values.at[spots[0]].set(low).at[spots[1]].set(largest)


def levels(rng, dims, cuts, low, high):
    def one(axis_at, blocks):
        steps = jax.random.uniform(jax.random.fold_in(jax.random.fold_in(rng, 6), axis_at), (blocks,), jnp.float32, low / len(cuts), high / len(cuts))
        return jnp.repeat(jnp.exp(steps), dims[axis_at] // blocks).reshape((-1,) + (1,) * (len(dims) - axis_at - 1))

    gain = one(*cuts[0])
    for cut in cuts[1:]:
        gain = gain * one(*cut)
    return gain


def setup_inputs(seed: int = 0) -> dict:
    key_of = jax.random.split(jax.random.key(seed), 8)
    hidden_states = draw_hidden_states(jax.random.fold_in(key_of[7], 71), 0)
    student_head = draw_student_head(jax.random.fold_in(key_of[7], 71), 0)
    teacher_probs = jnp.clip(jnp.exp(math.log(1.0) - 9.213757 * jax.random.uniform(key_of[2], (TOKENS, VT), jnp.float32) ** levels(key_of[2], (TOKENS, VT), ((1, 32),), -0.2, 0.2)), 9.965896606445312e-05, 1.0).astype(jnp.bfloat16)
    block_map = draw_block_map(jax.random.fold_in(key_of[7], 71), 0)
    context = plant(jax.random.randint(key_of[4], (NWIN,), 0, NCTX), jax.random.fold_in(key_of[4], 1), 0, NCTX - 1).astype(jnp.int32)
    map_gates = jnp.clip(jnp.exp(math.log(5.0) - 3.218876 * jax.random.uniform(key_of[5], (NCTX, NBS, K), jnp.float32) ** levels(key_of[5], (NCTX, NBS, K), ((1, 32),), -0.2, 0.2)), 0.2, 5.0)
    map_tiles = jnp.clip(jnp.exp(math.log(1.0) - 6.9083047 * jax.random.uniform(key_of[6], (NBS, K, BLK, BLK), jnp.float32) ** levels(key_of[6], (NBS, K, BLK, BLK), ((0, 32),), -0.2, 0.2)), 0.0009994507, 1.0).astype(jnp.bfloat16)
    return dict(hidden_states=hidden_states, student_head=student_head, teacher_probs=teacher_probs, block_map=block_map, context=context, map_gates=map_gates, map_tiles=map_tiles)


def reference(hidden_states, student_head, teacher_probs, block_map, context, map_gates, map_tiles):
    logits = jnp.dot(hidden_states, student_head, preferred_element_type=jnp.float32)
    peak = lax.optimization_barrier(jnp.max(logits, axis=1, keepdims=True))
    log_norm = peak + jnp.log(lax.optimization_barrier(jnp.sum(jnp.exp(logits - peak), axis=1, keepdims=True)))
    token_context = jnp.repeat(context, WIN)
    teacher_blocks = teacher_probs.reshape(TOKENS, NBT, BLK)
    gate_token = map_gates[token_context]
    stride = math.gcd(NBS, 16)

    def map_block(block_index):
        first_block = (block_index * stride).astype(jnp.int32)
        wanted = lax.dynamic_slice_in_dim(block_map, first_block, stride, 0)
        pieces = jnp.take(teacher_blocks, wanted.reshape(-1), axis=1).reshape(TOKENS, stride, K, BLK).astype(jnp.float32)
        tile_part = lax.dynamic_slice_in_dim(map_tiles, first_block, stride, 0).astype(jnp.float32)
        products = jnp.einsum('tbkj,bkjc->tbkc', pieces, tile_part)
        gate_part = lax.dynamic_slice_in_dim(gate_token, first_block, stride, 1)
        return lax.optimization_barrier(jnp.sum(gate_part[..., None] * products, axis=2))
    mapped = lax.map(map_block, jnp.arange(NBS // stride, dtype=jnp.int32))
    mapped = jnp.moveaxis(mapped, 0, 1).reshape(TOKENS, VS)
    row_total = lax.optimization_barrier(jnp.sum(mapped, axis=1, keepdims=True))
    target = mapped / row_total
    grad_logits = (VS * (jnp.exp(logits - log_norm) - target)).astype(jnp.bfloat16)
    kl_loss = jnp.sum(target * (jnp.log(target) - logits + log_norm)) / TOKENS
    inv_root = 1.0 / math.sqrt(TOKENS)
    column_width = math.gcd(VS, 4096)

    def grad_columns(column_index):
        first_column = (column_index * column_width).astype(jnp.int32)
        grad_part = lax.dynamic_slice_in_dim(grad_logits, first_column, column_width, 1)
        running = jnp.zeros((D, column_width), jnp.float32)
        for group in range(N_ROW):
            hidden_group = hidden_states[group * TOK_DEV:(group + 1) * TOK_DEV]
            grad_group = grad_part[group * TOK_DEV:(group + 1) * TOK_DEV]
            part_value = jnp.dot(hidden_group.T, grad_group, preferred_element_type=jnp.float32) * inv_root
            part_value = lax.optimization_barrier(part_value.astype(jnp.bfloat16))
            running = running + part_value.astype(jnp.float32)
        return running.astype(jnp.bfloat16)
    stacked = lax.map(grad_columns, jnp.arange(VS // column_width, dtype=jnp.int32))
    head_grad = jnp.moveaxis(stacked, 0, 1).reshape(D, VS)
    return (grad_logits, head_grad, kl_loss)
```

```python
import functools
import math

import jax
import jax.numpy as jnp
from jax import lax
from jax.experimental import pallas as pl
from jax.experimental.pallas import tpu as pltpu
from jax.sharding import PartitionSpec as P

MESH = pl.DeviceIdType.MESH
STEPS = 8


def route_tables(block_map, per_shard, voc_count, own_index):
    entries = block_map.size // voc_count
    wanted = block_map.reshape(voc_count, entries)
    sources = wanted // per_shard
    place = jnp.arange(entries, dtype=jnp.int32)
    big = entries * per_shard
    key = place[None, :] * per_shard + (wanted - sources * per_shard)
    owned = sources == own_index
    first = jnp.min(jnp.where(owned, key, big), axis=1)
    last = jnp.max(jnp.where(owned, key, -1), axis=1)
    take_first = first % per_shard
    take_second = jnp.where(last > first, last % per_shard, per_shard)
    mine = lax.dynamic_index_in_dim(sources, own_index, 0, keepdims=False)
    earlier = jnp.max(
        jnp.where((mine[None, :] == mine[:, None]) & (place[None, :] < place[:, None]), 1, 0), axis=1
    )
    slot_of = jnp.where(earlier > 0, voc_count, mine)
    slots = jnp.arange(voc_count + 1, dtype=jnp.int32)
    entry_of = jnp.max(jnp.where(slot_of[None, :] == slots[:, None], place[None, :], 0), axis=1)
    return take_first, take_second, slot_of, entry_of


def exchange_kernel(
    n,
    take_first,
    take_second,
    slot_of,
    entry_of,
    context_ref,
    gates_ref,
    hidden_ref,
    head_ref,
    teacher_ref,
    tiles_ref,
    logits_ref,
    mapped_ref,
    turned_ref,
    cols_ref,
    kl_ref,
    shelf,
    outgoing,
    incoming,
    extra,
    landing,
    products,
    stats_out,
    stats_in,
    send_sem,
    recv_sem,
    extra_send,
    extra_recv,
    stat_send,
    stat_recv,
):
    step = pl.program_id(0)
    me = lax.axis_index("voc")
    levels = n.bit_length() - 1
    bits = [(me // 2**b) % 2 for b in range(levels)]
    tokens, width = hidden_ref.shape
    block = tiles_ref.shape[-1]
    fanout = slot_of.shape[0] * block // mapped_ref.shape[1]
    chunk = head_ref.shape[1]
    windows = context_ref.shape[0]
    entries = slot_of.shape[0]

    def partner(d):
        return sum(((bits[b] + (d >> b)) % 2) * 2**b for b in range(levels))

    def reverse(e):
        return sum(((e // 2**b) % 2) * 2 ** (levels - 1 - b) for b in range(levels))

    order = sorted(range(1, n), reverse=True)

    def main_copy(d):
        return pltpu.make_async_remote_copy(
            src_ref=outgoing.at[partner(d)],
            dst_ref=incoming.at[me],
            send_sem=send_sem.at[d],
            recv_sem=recv_sem.at[d],
            device_id={"voc": partner(d)},
            device_id_type=MESH,
        )

    def main_recv(d):
        return pltpu.make_async_remote_copy(
            src_ref=outgoing.at[partner(d)],
            dst_ref=incoming.at[partner(d)],
            send_sem=send_sem.at[d],
            recv_sem=recv_sem.at[d],
            device_id={"voc": partner(d)},
            device_id_type=MESH,
        )

    def region(s):
        return sum(bits[b] * (n >> (b + 1)) for b in range(s))

    def extra_copy(s):
        half = n >> (s + 1)
        away = region(s) + (1 - bits[s]) * half
        return pltpu.make_async_remote_copy(
            src_ref=extra.at[pl.ds(away, half)],
            dst_ref=landing.at[pl.ds(n - 2 * half, half)],
            send_sem=extra_send.at[s],
            recv_sem=extra_recv.at[s],
            device_id={"voc": partner(1 << s)},
            device_id_type=MESH,
        )

    def extra_add(s):
        half = n >> (s + 1)
        kept = region(s) + bits[s] * half

        def add(i, carry):
            extra[kept + i] = extra[kept + i] + landing[n - 2 * half + i]
            return carry

        lax.fori_loop(0, half, add, 0)

    def stat_copy(d, owner):
        return pltpu.make_async_remote_copy(
            src_ref=stats_out,
            dst_ref=stats_in.at[owner],
            send_sem=stat_send.at[d],
            recv_sem=stat_recv.at[d],
            device_id={"voc": partner(d)},
            device_id_type=MESH,
        )

    @pl.when(step == 0)
    def _():
        barrier = pltpu.get_barrier_semaphore()
        for d in range(1, n):
            pl.semaphore_signal(barrier, inc=1, device_id={"voc": partner(d)}, device_id_type=MESH)

        def fill(e, carry):
            extra[reverse(e)] = shelf[take_second[e]]
            outgoing[e] = shelf[take_first[e]]
            return carry

        for i in range(shelf.shape[0] - 1):
            shelf[i] = teacher_ref[:, i * block : (i + 1) * block]
        shelf[shelf.shape[0] - 1] = jnp.zeros(shelf.shape[1:], shelf.dtype)

        lax.fori_loop(0, n, fill, 0)
        incoming[me] = outgoing[me]
        pl.semaphore_wait(barrier, n - 1)
        extra_copy(0).start()
        for d in order:
            main_copy(d).start()

    logits_ref[:, pl.ds(pl.multiple_of(step * chunk, chunk), chunk)] = jnp.dot(
        hidden_ref[...], head_ref[...], preferred_element_type=jnp.float32
    )
    rows = turned_ref.shape[0]
    turned_ref[...] = hidden_ref[:, pl.ds(pl.multiple_of(step * rows, rows), rows)].T

    for s in range(levels):

        @pl.when(step == s + 1)
        def _(s=s):
            extra_copy(s).wait()
            extra_add(s)
            if s + 1 < levels:
                extra_copy(s + 1).start()
            else:
                incoming[n] = extra[region(levels)]

    def multiply(slot):
        entry = entry_of[slot]
        value = jnp.dot(incoming[slot], tiles_ref[entry], preferred_element_type=jnp.float32)
        span = tokens // windows
        for w in range(windows):
            gate = gates_ref[context_ref[w] * entries + entry]
            products[slot, w * span : (w + 1) * span] = value[w * span : (w + 1) * span] * gate

    @pl.when(step == STEPS - 1)
    def _():
        peak = jnp.max(logits_ref[...], axis=1, keepdims=True)
        summed = jnp.sum(jnp.exp(logits_ref[...] - peak), axis=1, keepdims=True)
        multiply(me)
        multiply(n)
        for d in order:
            main_recv(d).wait_recv()
            multiply(partner(d))
        total = jnp.zeros((tokens, block), jnp.float32)
        cross = jnp.zeros((tokens, block), jnp.float32)
        for b in range(entries // fanout):
            value = products[slot_of[b * fanout]]
            for k in range(1, fanout):
                value = value + products[slot_of[b * fanout + k]]
            mapped_ref[:, b * block : (b + 1) * block] = value
            total = total + value
            cross = cross + value * (
                jnp.log(value) - (logits_ref[:, b * block : (b + 1) * block] - peak)
            )
        total = jnp.sum(total, axis=1, keepdims=True)
        cross = jnp.sum(cross, axis=1, keepdims=True)
        lane = lax.broadcasted_iota(jnp.int32, (tokens, block), 1)
        packed = jnp.where(
            lane == 0, peak, jnp.where(lane == 1, summed, jnp.where(lane == 2, total, cross))
        )
        stats_out[...] = packed.T[:8]
        stats_in[me] = stats_out[...]
        for d in order:
            stat_copy(d, me).start()
        for d in order:
            stat_copy(d, partner(d)).wait_recv()
        peaks = stats_in[:, 0, :]
        sums = stats_in[:, 1, :]
        totals = stats_in[:, 2, :]
        crosses = stats_in[:, 3, :]
        top = jnp.max(peaks, axis=0, keepdims=True)
        log_norm = top + jnp.log(jnp.sum(sums * jnp.exp(peaks - top), axis=0, keepdims=True))
        row_total = jnp.sum(totals, axis=0, keepdims=True)
        weighted = jnp.sum(crosses + totals * (log_norm - peaks), axis=0, keepdims=True)
        divergence = weighted / row_total - jnp.log(row_total)
        kl_ref[...] = jnp.broadcast_to(jnp.sum(divergence, axis=1, keepdims=True), kl_ref.shape)
        line = lax.broadcasted_iota(jnp.int32, (block, tokens), 0)
        cols_ref[...] = jnp.where(line == 0, log_norm, 1.0 / row_total).T
        for d in order:
            main_copy(d).wait_send()
            stat_copy(d, me).wait_send()


def exchange(hidden, head, teacher, tables, context, gates, tiles):
    n = lax.axis_size("voc")
    tokens, width = hidden.shape
    cols = head.shape[1]
    block = tiles.shape[-1]
    levels = n.bit_length() - 1
    smem = pl.BlockSpec(memory_space=pltpu.SMEM)

    def whole(shape):
        return pl.BlockSpec(shape, lambda i: (0,) * len(shape), pipeline_mode=pl.Buffered(1))

    return pl.pallas_call(
        functools.partial(exchange_kernel, n),
        grid=(STEPS,),
        out_shape=(
            jax.ShapeDtypeStruct((tokens, cols), jnp.float32),
            jax.ShapeDtypeStruct((tokens, cols), jnp.float32),
            jax.ShapeDtypeStruct((width, tokens), hidden.dtype),
            jax.ShapeDtypeStruct((tokens, block), jnp.float32),
            jax.ShapeDtypeStruct((8, 128), jnp.float32),
        ),
        in_specs=[smem] * 6
        + [
            whole((tokens, width)),
            pl.BlockSpec((width, cols // STEPS), lambda i: (0, i)),
            whole(teacher.shape),
            whole(tiles.shape),
        ],
        out_specs=(
            whole((tokens, cols)),
            whole((tokens, cols)),
            pl.BlockSpec((width // STEPS, tokens), lambda i: (i, 0)),
            whole((tokens, block)),
            whole((8, 128)),
        ),
        scratch_shapes=[
            pltpu.VMEM((teacher.shape[1] // block + 1, tokens, block), teacher.dtype),
            pltpu.VMEM((n, tokens, block), teacher.dtype),
            pltpu.VMEM((n + 1, tokens, block), teacher.dtype),
            pltpu.VMEM((n, tokens, block), teacher.dtype),
            pltpu.VMEM((n, tokens, block), teacher.dtype),
            pltpu.VMEM((n + 1, tokens, block), jnp.float32),
            pltpu.VMEM((8, tokens), jnp.float32),
            pltpu.VMEM((n, 8, tokens), jnp.float32),
            pltpu.SemaphoreType.DMA((n,)),
            pltpu.SemaphoreType.DMA((n,)),
            pltpu.SemaphoreType.DMA((levels,)),
            pltpu.SemaphoreType.DMA((levels,)),
            pltpu.SemaphoreType.DMA((n,)),
            pltpu.SemaphoreType.DMA((n,)),
        ],
        compiler_params=pltpu.CompilerParams(
            collective_id=0, has_side_effects=True, vmem_limit_bytes=48 << 20
        ),
        name="exchange",
    )(*tables, context, gates, hidden, head, teacher, tiles)


def gradient_kernel(vocab, inv_root, cols_ref, logits_ref, mapped_ref, turned_ref, grad_ref, out_ref):
    log_norm = cols_ref[:, 0:1]
    inverse = cols_ref[:, 1:2]
    grad = (
        vocab * (jnp.exp(logits_ref[...] - log_norm) - mapped_ref[...] * inverse)
    ).astype(grad_ref.dtype)
    grad_ref[...] = grad
    out_ref[...] = (
        jnp.dot(turned_ref[...], grad, preferred_element_type=jnp.float32) * inv_root
    ).astype(out_ref.dtype)


def gradients(logits, mapped, turned, cols, vocab, inv_root):
    tokens, columns = logits.shape
    width = turned.shape[0]
    chunk = columns // STEPS
    part = pl.BlockSpec((tokens, chunk), lambda i: (0, i))
    return pl.pallas_call(
        functools.partial(gradient_kernel, float(vocab), inv_root),
        grid=(STEPS,),
        out_shape=(
            jax.ShapeDtypeStruct((tokens, columns), jnp.bfloat16),
            jax.ShapeDtypeStruct((width, columns), jnp.bfloat16),
        ),
        in_specs=[
            pl.BlockSpec(cols.shape, lambda i: (0, 0), pipeline_mode=pl.Buffered(1)),
            part,
            part,
            pl.BlockSpec(turned.shape, lambda i: (0, 0), pipeline_mode=pl.Buffered(1)),
        ],
        out_specs=(part, pl.BlockSpec((width, chunk), lambda i: (0, i))),
        compiler_params=pltpu.CompilerParams(vmem_limit_bytes=32 << 20),
        name="gradients",
    )(cols, logits, mapped, turned)


def per_device(
    hidden_states, student_head, teacher_probs, block_map, context, map_gates, map_tiles
):
    voc_count = lax.axis_size("voc")
    own_index = lax.axis_index("voc")
    rows_total = hidden_states.shape[0] * lax.axis_size("row")
    inv_root = 1.0 / math.sqrt(rows_total)
    vocab_total = student_head.shape[1] * voc_count
    blocks, fanout, block, _ = map_tiles.shape
    head = lax.all_gather(student_head, "row", axis=0, tiled=True)
    tables = route_tables(block_map, teacher_probs.shape[1] // block, voc_count, own_index)
    logits, mapped, turned, cols, kl = exchange(
        hidden_states,
        head,
        teacher_probs,
        tables,
        context,
        map_gates.reshape(-1),
        map_tiles.reshape(blocks * fanout, block, block),
    )
    grad_logits, head_part = gradients(logits, mapped, turned, cols, vocab_total, inv_root)
    kl_loss = lax.psum(kl[0, 0], "row") / rows_total
    head_grad = lax.psum_scatter(head_part, "row", scatter_dimension=0, tiled=True)
    return (grad_logits, head_grad, kl_loss)


def solution(mesh):
    placed = (
        P("row", None),
        P("row", "voc"),
        P("row", "voc"),
        P(),
        P("row"),
        P(None, "voc", None),
        P("voc", None, None, None),
    )
    return jax.shard_map(
        per_device,
        mesh=mesh,
        in_specs=placed,
        out_specs=(P("row", "voc"), P("row", "voc"), P()),
        check_vma=False,
    )
```

```python
import functools
import math

import jax
import jax.numpy as jnp
from jax import lax
from jax.experimental import pallas as pl
from jax.experimental.pallas import tpu as pltpu
from jax.sharding import PartitionSpec as P

MESH = pl.DeviceIdType.MESH
STEPS = 8


def route_tables(block_map, per_shard, voc_count, own_index):
    entries = block_map.size // voc_count
    wanted = block_map.reshape(voc_count, entries)
    sources = wanted // per_shard
    place = jnp.arange(entries, dtype=jnp.int32)
    big = entries * per_shard
    key = place[None, :] * per_shard + (wanted - sources * per_shard)
    owned = sources == own_index
    first = jnp.min(jnp.where(owned, key, big), axis=1)
    last = jnp.max(jnp.where(owned, key, -1), axis=1)
    take_first = first % per_shard
    take_second = jnp.where(last > first, last % per_shard, per_shard)
    mine = lax.dynamic_index_in_dim(sources, own_index, 0, keepdims=False)
    earlier = jnp.max(
        jnp.where((mine[None, :] == mine[:, None]) & (place[None, :] < place[:, None]), 1, 0), axis=1
    )
    slot_of = jnp.where(earlier > 0, voc_count, mine)
    slots = jnp.arange(voc_count + 1, dtype=jnp.int32)
    entry_of = jnp.max(jnp.where(slot_of[None, :] == slots[:, None], place[None, :], 0), axis=1)
    return take_first, take_second, slot_of, entry_of


def exchange_kernel(
    n,
    take_first,
    take_second,
    slot_of,
    entry_of,
    context_ref,
    gates_ref,
    hidden_hbm,
    head_ref,
    teacher_ref,
    tiles_hbm,
    logits_hbm,
    mapped_hbm,
    turned_ref,
    cols_ref,
    hidden_ref,
    tiles_ref,
    logits_ref,
    mapped_ref,
    local_sem,
    shelf,
    outgoing,
    incoming,
    extra,
    landing,
    products,
    stats_out,
    stats_in,
    send_sem,
    recv_sem,
    extra_send,
    extra_recv,
    stat_send,
    stat_recv,
):
    step = pl.program_id(0)
    me = lax.axis_index("voc")
    levels = n.bit_length() - 1
    bits = [(me // 2**b) % 2 for b in range(levels)]
    tokens, width = hidden_ref.shape
    block = tiles_ref.shape[-1]
    fanout = slot_of.shape[0] * block // mapped_ref.shape[1]
    chunk = head_ref.shape[1]
    windows = context_ref.shape[0]
    entries = slot_of.shape[0]

    def partner(d):
        return sum(((bits[b] + (d >> b)) % 2) * 2**b for b in range(levels))

    def reverse(e):
        return sum(((e // 2**b) % 2) * 2 ** (levels - 1 - b) for b in range(levels))

    half_count = n // 2
    order = [
        d for d in reversed(range(1, n))
    ]
    batch = -(-len(order) // levels)
    late = {s: min(batch * (3 * s - 8), n - 2) for s in range(3, levels)}
    load_hidden = pltpu.make_async_copy(hidden_hbm, hidden_ref, local_sem.at[0])
    load_tiles = pltpu.make_async_copy(tiles_hbm, tiles_ref, local_sem.at[1])
    save_logits = pltpu.make_async_copy(logits_ref, logits_hbm, local_sem.at[2])
    save_mapped = pltpu.make_async_copy(mapped_ref, mapped_hbm, local_sem.at[3])

    def main_copy(d):
        return pltpu.make_async_remote_copy(
            src_ref=outgoing.at[partner(d)],
            dst_ref=incoming.at[me],
            send_sem=send_sem.at[d],
            recv_sem=recv_sem.at[d],
            device_id={"voc": partner(d)},
            device_id_type=MESH,
        )

    def main_recv(d):
        return pltpu.make_async_remote_copy(
            src_ref=outgoing.at[partner(d)],
            dst_ref=incoming.at[partner(d)],
            send_sem=send_sem.at[d],
            recv_sem=recv_sem.at[d],
            device_id={"voc": partner(d)},
            device_id_type=MESH,
        )

    def region(s):
        return sum(bits[b] * (n >> (b + 1)) for b in range(s))

    def extra_copy(s):
        half = n >> (s + 1)
        away = region(s) + (1 - bits[s]) * half
        return pltpu.make_async_remote_copy(
            src_ref=extra.at[pl.ds(away, half)],
            dst_ref=landing.at[pl.ds(n - 2 * half, half)],
            send_sem=extra_send.at[s],
            recv_sem=extra_recv.at[s],
            device_id={"voc": partner(1 << s)},
            device_id_type=MESH,
        )

    def extra_add(s):
        half = n >> (s + 1)
        kept = region(s) + bits[s] * half

        def add(i, carry):
            extra[kept + i] = extra[kept + i] + landing[n - 2 * half + i]
            return carry

        lax.fori_loop(0, half, add, 0)

    def stat_copy(d, owner):
        return pltpu.make_async_remote_copy(
            src_ref=stats_out,
            dst_ref=stats_in.at[owner],
            send_sem=stat_send.at[d],
            recv_sem=stat_recv.at[d],
            device_id={"voc": partner(d)},
            device_id_type=MESH,
        )

    def send_batch(s):
        for d in order[s * batch : (s + 1) * batch]:
            main_copy(d).start()

    def extra_finish(s):
        extra_copy(s).wait()
        extra_add(s)
        if s + 1 < levels:
            extra_copy(s + 1).start()
            send_batch(s + 1)
        else:
            incoming[n] = extra[region(levels)]

    @pl.when(step == 0)
    def _():
        load_hidden.start()
        barrier = pltpu.get_barrier_semaphore()
        for d in range(1, n):
            pl.semaphore_signal(barrier, inc=1, device_id={"voc": partner(d)}, device_id_type=MESH)

        def fill(e, carry):
            extra[reverse(e)] = shelf[take_second[e]]
            outgoing[e] = shelf[take_first[e]]
            return carry

        for i in range(shelf.shape[0] - 1):
            shelf[i] = teacher_ref[:, i * block : (i + 1) * block]
        shelf[shelf.shape[0] - 1] = jnp.zeros(shelf.shape[1:], shelf.dtype)

        lax.fori_loop(0, n, fill, 0)
        incoming[me] = outgoing[me]
        pl.semaphore_wait(barrier, n - 1)
        extra_copy(0).start()
        send_batch(0)
        load_tiles.start()
        load_hidden.wait()

    logits_ref[:, pl.ds(pl.multiple_of(step * chunk, chunk), chunk)] = jnp.dot(
        hidden_ref[...], head_ref[...], preferred_element_type=jnp.float32
    )
    rows = turned_ref.shape[0]
    turned_ref[...] = hidden_ref[:, pl.ds(pl.multiple_of(step * rows, rows), rows)].T

    for s in range(min(levels, 3)):

        @pl.when(step == (1, 3, 6)[s])
        def _(s=s):
            extra_finish(s)

    def multiply(slot):
        entry = entry_of[slot]
        value = jnp.dot(incoming[slot], tiles_ref[entry], preferred_element_type=jnp.float32)
        span = tokens // windows
        for w in range(windows):
            gate = gates_ref[context_ref[w] * entries + entry]
            products[slot, w * span : (w + 1) * span] = value[w * span : (w + 1) * span] * gate

    @pl.when(step == STEPS - 1)
    def _():
        save_logits.start()
        load_tiles.wait()
        peak = jnp.max(logits_ref[...], axis=1, keepdims=True)
        summed = jnp.sum(jnp.exp(logits_ref[...] - peak), axis=1, keepdims=True)
        multiply(me)
        for i, d in enumerate(order):
            main_recv(d).wait_recv()
            multiply(partner(d))
            for s in late:
                if late[s] == i:
                    extra_finish(s)
        multiply(n)
        total = jnp.zeros((tokens, block), jnp.float32)
        cross = jnp.zeros((tokens, block), jnp.float32)
        for b in range(entries // fanout):
            value = products[slot_of[b * fanout]]
            for k in range(1, fanout):
                value = value + products[slot_of[b * fanout + k]]
            mapped_ref[:, b * block : (b + 1) * block] = value
            total = total + value
            cross = cross + value * (
                jnp.log(value) - (logits_ref[:, b * block : (b + 1) * block] - peak)
            )
        save_mapped.start()
        total = jnp.sum(total, axis=1, keepdims=True)
        cross = jnp.sum(cross, axis=1, keepdims=True)
        lane = lax.broadcasted_iota(jnp.int32, (tokens, block), 1)
        packed = jnp.where(
            lane == 0, peak, jnp.where(lane == 1, summed, jnp.where(lane == 2, total, cross))
        )
        stats_out[...] = packed.T[:8]
        stats_in[me] = stats_out[...]
        for d in order:
            stat_copy(d, me).start()
        for d in order:
            stat_copy(d, partner(d)).wait_recv()
        peaks = stats_in[:, 0, :]
        sums = stats_in[:, 1, :]
        totals = stats_in[:, 2, :]
        crosses = stats_in[:, 3, :]
        top = jnp.max(peaks, axis=0, keepdims=True)
        log_norm = top + jnp.log(jnp.sum(sums * jnp.exp(peaks - top), axis=0, keepdims=True))
        row_total = jnp.sum(totals, axis=0, keepdims=True)
        weighted = jnp.sum(crosses + totals * (log_norm - peaks), axis=0, keepdims=True)
        divergence = weighted / row_total - jnp.log(row_total)
        divergence = jnp.sum(divergence, axis=1, keepdims=True)
        line = lax.broadcasted_iota(jnp.int32, (block, tokens), 0)
        cols_ref[...] = jnp.where(
            line == 0, log_norm, jnp.where(line == 1, 1.0 / row_total, divergence)
        ).T
        for d in order:
            main_copy(d).wait_send()
            stat_copy(d, me).wait_send()
        save_logits.wait()
        save_mapped.wait()


def exchange(hidden, head, teacher, tables, context, gates, tiles):
    n = lax.axis_size("voc")
    tokens, width = hidden.shape
    cols = head.shape[1]
    block = tiles.shape[-1]
    levels = n.bit_length() - 1
    hbm = pl.BlockSpec(memory_space=pl.ANY)
    smem = pl.BlockSpec(memory_space=pltpu.SMEM)

    def whole(shape):
        return pl.BlockSpec(shape, lambda i: (0,) * len(shape), pipeline_mode=pl.Buffered(1))

    return pl.pallas_call(
        functools.partial(exchange_kernel, n),
        grid=(STEPS,),
        out_shape=(
            jax.ShapeDtypeStruct((tokens, cols), jnp.float32),
            jax.ShapeDtypeStruct((tokens, cols), jnp.float32),
            jax.ShapeDtypeStruct((width, tokens), hidden.dtype),
            jax.ShapeDtypeStruct((tokens, block), jnp.float32),
        ),
        in_specs=[smem] * 6
        + [
            hbm,
            pl.BlockSpec((width, cols // STEPS), lambda i: (0, i)),
            whole(teacher.shape),
            hbm,
        ],
        out_specs=(
            hbm,
            hbm,
            pl.BlockSpec((width // STEPS, tokens), lambda i: (i, 0)),
            whole((tokens, block)),
        ),
        scratch_shapes=[
            pltpu.VMEM((tokens, width), hidden.dtype),
            pltpu.VMEM(tiles.shape, tiles.dtype),
            pltpu.VMEM((tokens, cols), jnp.float32),
            pltpu.VMEM((tokens, cols), jnp.float32),
            pltpu.SemaphoreType.DMA((4,)),
            pltpu.VMEM((teacher.shape[1] // block + 1, tokens, block), teacher.dtype),
            pltpu.VMEM((n, tokens, block), teacher.dtype),
            pltpu.VMEM((n + 1, tokens, block), teacher.dtype),
            pltpu.VMEM((n, tokens, block), teacher.dtype),
            pltpu.VMEM((n, tokens, block), teacher.dtype),
            pltpu.VMEM((n + 1, tokens, block), jnp.float32),
            pltpu.VMEM((8, tokens), jnp.float32),
            pltpu.VMEM((n, 8, tokens), jnp.float32),
            pltpu.SemaphoreType.DMA((n,)),
            pltpu.SemaphoreType.DMA((n,)),
            pltpu.SemaphoreType.DMA((levels,)),
            pltpu.SemaphoreType.DMA((levels,)),
            pltpu.SemaphoreType.DMA((n,)),
            pltpu.SemaphoreType.DMA((n,)),
        ],
        compiler_params=pltpu.CompilerParams(
            collective_id=0, has_side_effects=True, vmem_limit_bytes=60 << 20
        ),
        name="exchange",
    )(*tables, context, gates, hidden, head, teacher, tiles)


def gradient_kernel(
    vocab, inv_root, rows, cols_ref, logits_ref, mapped_ref, turned_ref, grad_ref, out_ref, kl_ref
):
    @pl.when(pl.program_id(0) == 0)
    def _():
        kl_ref[0, 0] = cols_ref[0, 2] * (1.0 / rows)

    log_norm = cols_ref[:, 0:1]
    inverse = cols_ref[:, 1:2]
    grad = (
        vocab * (jnp.exp(logits_ref[...] - log_norm) - mapped_ref[...] * inverse)
    ).astype(grad_ref.dtype)
    grad_ref[...] = grad
    out_ref[...] = (
        jnp.dot(turned_ref[...], grad, preferred_element_type=jnp.float32) * inv_root
    ).astype(out_ref.dtype)


def gradients(logits, mapped, turned, cols, vocab, inv_root, rows):
    tokens, columns = logits.shape
    width = turned.shape[0]
    chunk = columns // STEPS
    part = pl.BlockSpec((tokens, chunk), lambda i: (0, i))
    return pl.pallas_call(
        functools.partial(gradient_kernel, float(vocab), inv_root, rows),
        grid=(STEPS,),
        out_shape=(
            jax.ShapeDtypeStruct((tokens, columns), jnp.bfloat16),
            jax.ShapeDtypeStruct((width, columns), jnp.bfloat16),
            jax.ShapeDtypeStruct((1, 1), jnp.float32),
        ),
        in_specs=[
            pl.BlockSpec(cols.shape, lambda i: (0, 0), pipeline_mode=pl.Buffered(1)),
            part,
            part,
            pl.BlockSpec(turned.shape, lambda i: (0, 0), pipeline_mode=pl.Buffered(1)),
        ],
        out_specs=(
            part,
            pl.BlockSpec((width, chunk), lambda i: (0, i)),
            pl.BlockSpec(memory_space=pltpu.SMEM),
        ),
        compiler_params=pltpu.CompilerParams(vmem_limit_bytes=60 << 20),
        name="gradients",
    )(cols, logits, mapped, turned)


def per_device(
    hidden_states, student_head, teacher_probs, block_map, context, map_gates, map_tiles
):
    voc_count = lax.axis_size("voc")
    own_index = lax.axis_index("voc")
    rows_total = hidden_states.shape[0] * lax.axis_size("row")
    inv_root = 1.0 / math.sqrt(rows_total)
    vocab_total = student_head.shape[1] * voc_count
    blocks, fanout, block, _ = map_tiles.shape
    head = lax.all_gather(student_head, "row", axis=0, tiled=True)
    tables = route_tables(block_map, teacher_probs.shape[1] // block, voc_count, own_index)
    logits, mapped, turned, cols = exchange(
        hidden_states,
        head,
        teacher_probs,
        tables,
        context,
        map_gates.reshape(-1),
        map_tiles.reshape(blocks * fanout, block, block),
    )
    grad_logits, head_part, kl = gradients(
        logits, mapped, turned, cols, vocab_total, inv_root, rows_total
    )
    kl_loss = lax.psum(kl.reshape(()), "row")
    head_grad = lax.psum_scatter(head_part, "row", scatter_dimension=0, tiled=True)
    return (grad_logits, head_grad, kl_loss)


def solution(mesh):
    placed = (
        P("row", None),
        P("row", "voc"),
        P("row", "voc"),
        P(),
        P("row"),
        P(None, "voc", None),
        P("voc", None, None, None),
    )
    return jax.shard_map(
        per_device,
        mesh=mesh,
        in_specs=placed,
        out_specs=(P("row", "voc"), P("row", "voc"), P()),
        check_vma=False,
    )
```
